256 devices in a mesh: tok: 8 (over x, core), wa: 32 (over z, y).
Axes of the slice: x: 4, y: 4, z: 8, core: 2. Of those that a mesh axis runs over, the one named last changes fastest.
Arguments:
- tokens: bfloat16 [4096, 8192], P('tok', 'wa'), may hold values from -6 to 6
- gate_weight: bfloat16 [224, 8, 128, 128], P('wa', 'tok'), may hold values from -0.1875 to 0.1875
- up_weight: bfloat16 [224, 8, 128, 128], P('wa', 'tok'), may hold values from -0.1875 to 0.1875
- down_weight: bfloat16 [64, 24, 128, 128], P('wa', 'tok'), may hold values from -0.109375 to 0.109375
- gate_list: int32 [224, 8], P('wa'), may hold values from -1 to 63, as said below
- up_list: int32 [224, 8], P('wa'), may hold values from -1 to 63, as said below
- down_list: int32 [64, 24], replicated, may hold values from -1 to 223, as said below
Outputs:
- mixed_out: bfloat16 [4096, 8192], P('tok', 'wa')
The draws below stay inside these ranges and needn't reach their ends.
Inputs may be any that keep to these rules, and one draw needn't show every extreme that they name: `gate_list`: row j lists distinct feature blocks in ascending order followed by -1; each row has 4 to 8 entries and some row exactly 8. `up_list`: row j lists distinct feature blocks in ascending order followed by -1; each row has 4 to 8 entries and some row exactly 8. `down_list`: row c lists distinct hidden blocks in ascending order followed by -1; each row has 18 to 24 entries and some row exactly 24. Each aligned group of 2 rows names at most 2 distinct blocks of any aligned range of 7 hidden blocks, and every group names exactly 2 of some range.
All inputs are finite; a program needn't handle non-finite values.
Results may differ from the reference program's by a relative error of at most 0.0049.
Values may be sent and summed in bfloat16 or wider, within the bound.
No kernel may reach another device: no remote copies, remote signals or barrier semaphores. Data moves between devices by JAX's collectives and lax.ppermute only.
A program may use at most 128 MiB of HBM per device.

```python
import jax
import jax.numpy as jnp
from jax import lax

D = 8192
BLK = 128
KG = 8
KD = 24
TOKENS = 4096
ROWB = 64
HIDB = 224
HB_DEV = 7
DB_DEV = 2
CAP = 2


def column_lists(key, columns, choices, width):
    score_key, count_key = jax.random.split(key)
    scores = jax.random.randint(score_key, (columns, choices), 0, 1 << 20) * choices
    scores = scores + jnp.arange(choices, dtype=jnp.int32)[None, :]
    top_values, chosen = lax.top_k(scores, width)
    chosen = jnp.sort(chosen.astype(jnp.int32), axis=1)
    counts = jax.random.randint(count_key, (columns,), width // 2, width + 1)
    counts = counts.at[0].set(width)
    keep = jnp.arange(width, dtype=jnp.int32)[None, :] < counts[:, None]
    return jnp.where(keep, chosen, -1).astype(jnp.int32)


def draw_gate_list(key, part):
    return column_lists(jax.random.fold_in(key, 11), HIDB, ROWB, KG)


def draw_up_list(key, part):
    return column_lists(jax.random.fold_in(key, 12), HIDB, ROWB, KG)


def draw_down_list(key, part):
    owners = HIDB // HB_DEV
    groups = ROWB // DB_DEV
    pool_key, pick_key, count_key = jax.random.split(jax.random.fold_in(key, 13), 3)
    pool_scores = jax.random.randint(pool_key, (groups, owners, HB_DEV), 0, 1 << 20) * HB_DEV
    pool_scores = pool_scores + jnp.arange(HB_DEV, dtype=jnp.int32)[None, None, :]
    pool_values, local_ids = lax.top_k(pool_scores, CAP)
    owner_base = jnp.arange(owners, dtype=jnp.int32)[None, :, None] * HB_DEV
    pool = (local_ids.astype(jnp.int32) + owner_base).reshape(groups, owners * CAP)
    pool_size = owners * CAP
    forced = (jnp.arange(groups, dtype=jnp.int32) + 1) % owners
    slot_owner = jnp.arange(pool_size, dtype=jnp.int32) // CAP
    first_column = (jnp.arange(DB_DEV, dtype=jnp.int32) == 0)[None, :, None]
    boost = ((slot_owner[None, :] == forced[:, None])[:, None, :] & first_column).astype(jnp.int32)
    scores = jax.random.randint(pick_key, (groups, DB_DEV, pool_size), 0, 1 << 20) * pool_size
    scores = scores + jnp.arange(pool_size, dtype=jnp.int32)[None, None, :] + boost * (1 << 29)
    pick_values, chosen = lax.top_k(scores, KD)
    expanded = jnp.broadcast_to(pool[:, None, :], (groups, DB_DEV, pool_size))
    named = jnp.take_along_axis(expanded, chosen.astype(jnp.int32), axis=2)
    named = jnp.sort(named, axis=2)
    counts = jax.random.randint(count_key, (groups, DB_DEV), 3 * KD // 4, KD + 1)
    counts = counts.at[:, 0].set(KD)
    keep = jnp.arange(KD, dtype=jnp.int32)[None, None, :] < counts[:, :, None]
    return jnp.where(keep, named, -1).reshape(ROWB, KD).astype(jnp.int32)


def levels(own_key, dims, shards, low, high):
    loudness, own = 1.0, jax.random.fold_in(own_key, 6)
    for position, parts in shards:
        steps = jnp.exp(jax.random.uniform(jax.random.fold_in(own, position), (parts,), jnp.float32, low / len(shards), high / len(shards)))
        loudness = loudness * jnp.repeat(steps, dims[position] // parts).reshape([-1 if axis == position else 1 for axis in range(len(dims))])
    return loudness


def scatter_about(own_key, extent, spread, bound, cuts=(), kind=jnp.bfloat16):
    level = levels(own_key, extent, cuts, -0.22, 0.18) if cuts else 1.0
    result = jax.random.normal(own_key, extent, jnp.float32) * spread * level
    return jnp.minimum(jnp.maximum(result, -bound), bound).astype(kind)


def setup_inputs(seed: int = 0) -> dict:
    splits = jax.random.split(jax.random.key(seed), 8)
    tokens = scatter_about(splits[0], (TOKENS, D), 1.0, 6.0, ((0, 8), (1, 32)))
    gate_weight = scatter_about(splits[1], (HIDB, KG, BLK, BLK), (KG * BLK) ** -0.5, 0.1875, ((0, 32), (1, 8)))
    up_weight = scatter_about(splits[2], (HIDB, KG, BLK, BLK), (KG * BLK) ** -0.5, 0.1875, ((0, 32), (1, 8)))
    down_weight = scatter_about(splits[3], (ROWB, KD, BLK, BLK), (KD * BLK) ** -0.5, 0.109375, ((0, 32), (1, 8)))
    gate_list = draw_gate_list(jax.random.fold_in(splits[7], 71), 0)
    up_list = draw_up_list(jax.random.fold_in(splits[7], 71), 0)
    down_list = draw_down_list(jax.random.fold_in(splits[7], 71), 0)
    return {"tokens": tokens, "gate_weight": gate_weight, "up_weight": up_weight, "down_weight": down_weight, "gate_list": gate_list, "up_list": up_list, "down_list": down_list}


def listed_sum(sources, weights, block_list):
    present = (block_list >= 0).astype(jnp.float32)
    picked = jnp.take(sources, jnp.maximum(block_list, 0), axis=0).astype(jnp.float32)
    picked = picked * present[:, None, None]
    return jnp.einsum("ktm,kmn->tn", picked, weights.astype(jnp.float32))


def reference(tokens, gate_weight, up_weight, down_weight, gate_list, up_list, down_list):
    feature_blocks = jnp.transpose(tokens.reshape(TOKENS, ROWB, BLK), (1, 0, 2))

    def hidden_block(operands):
        gate_w, up_w, gate_l, up_l = operands
        gate_sum = listed_sum(feature_blocks, gate_w, gate_l)
        up_sum = listed_sum(feature_blocks, up_w, up_l)
        return (jax.nn.silu(gate_sum) * up_sum).astype(jnp.bfloat16)

    hidden = lax.map(hidden_block, (gate_weight, up_weight, gate_list, up_list))

    def output_block(operands):
        down_w, down_l = operands
        return listed_sum(hidden, down_w, down_l).astype(jnp.bfloat16)

    mixed_out = lax.map(output_block, (down_weight, down_list))
    return jnp.transpose(mixed_out, (1, 0, 2)).reshape(TOKENS, ROWB * BLK)
```

```python
import jax
import jax.numpy as jnp
from jax import lax
from jax.experimental import pallas as pl
from jax.experimental.pallas import tpu as pltpu
from jax.sharding import Mesh, PartitionSpec as P


NX, NC, NZ, NY = 4, 2, 8, 4
RA = 288
BF, F32 = jnp.bfloat16, jnp.float32
ANY = pl.BlockSpec(memory_space=pl.ANY)
SMEM = pl.BlockSpec(memory_space=pltpu.SMEM)


def shift(value, axis, by):
    size = {"x": NX, "c": NC, "z": NZ, "y": NY}[axis]
    return lax.ppermute(value, axis, [(i, (i + by) % size) for i in range(size)])


def cut(parts, start, stop):
    found, base = [], 0
    for part in parts:
        rows = part.shape[0]
        lo, hi = max(start, base), min(stop, base + rows)
        if lo < hi:
            found.append((part, lo - base, hi - lo))
        base += rows
    return found


def pack(pieces, shape):
    arrays = []
    for array, *_ in pieces:
        if not any(array is known for known in arrays):
            arrays.append(array)

    def body(*refs):
        out, sem = refs[-2:]
        copies = []
        for i, (array, at, to) in enumerate(pieces):
            src = refs[[array is known for known in arrays].index(True)].at[at]
            copies.append(pltpu.make_async_copy(src, out.at[to], sem.at[i]))
        for c in copies:
            c.start()
        for c in copies:
            c.wait()

    return pl.pallas_call(
        body,
        out_shape=jax.ShapeDtypeStruct(shape, BF),
        in_specs=[ANY] * len(arrays),
        out_specs=pl.BlockSpec(memory_space=pltpu.VMEM),
        scratch_shapes=[pltpu.SemaphoreType.DMA((len(pieces),))],
    )(*arrays)


def rows_of(parts, start, stop, row):
    out = []
    for part, lo, count in cut(parts, start, stop):
        out.append((part, (pl.ds(lo, count), slice(None)), (pl.ds(row, count), slice(None))))
        row += count
    return out


def tables(meta, gates, ups, downs, pos, hpos, first, last):
    z, y = meta[2], meta[3]
    base = z * 28

    def feature(r, carry):
        for which, lists in enumerate((gates, ups)):
            for i in range(8):
                f = lists[r, i]
                g = jnp.maximum(f, 0)
                owner = g >> 1
                piece = ((z + 8 - (owner >> 2)) & 7) * 4 + ((y + 4 - (owner & 3)) & 3)
                pos[(which * 7 + r) * 8 + i] = jnp.where(f >= 0, 2 * piece + (g & 1), -1)
        return carry

    lax.fori_loop(0, 7, feature, 0)

    def column(r, carry):
        row = ((r >> 1) * 4 + y) * 2 + (r & 1)
        below = upto = jnp.int32(0)
        for k in range(24):
            h = downs[row, k]
            local = h - base
            listed = (h >= 0).astype(jnp.int32)
            below += jnp.where(local < 0, listed, 0)
            upto += jnp.where(local < 28, listed, 0)
            local = jnp.clip(local, 0, 27)
            source = (local * 37) >> 8
            hpos[r * 24 + k] = ((y + 4 - source) & 3) * 7 + local - 7 * source
        first[r] = below
        last[r] = upto
        return carry

    lax.fori_loop(0, 16, column, 0)


def hidden_kernel(plan, n_feat, n_w, blocks, slots):
    def body(meta, pos, *refs):
        feats, weights = refs[:n_feat], refs[n_feat : n_feat + n_w]
        out, fbuf, wbuf, fsem, wsem = refs[n_feat + n_w :]
        copies = []
        for ref, lo, count, piece, dst in plan["feat"]:
            for h in range(2):
                copies.append(
                    pltpu.make_async_copy(
                        feats[ref].at[pl.ds(lo, count), pl.ds(h * 128, 128)],
                        fbuf.at[2 * piece + h, pl.ds(dst, count), :],
                        fsem.at[len(copies)],
                    )
                )
        loads = []
        for i, (ref, row, q, count) in enumerate(plan["weight"]):
            loads.append(pltpu.make_async_copy(weights[ref].at[pl.ds(row, count)], wbuf.at[q], wsem.at[i]))
        for c in loads + copies:
            c.start()
        x, core = meta[0], meta[1]
        for c in loads + copies:
            c.wait()

        def product(j, which):
            total = None
            for pair in range(slots // 2):
                left, right = [], []
                for q in (2 * pair, 2 * pair + 1):
                    dc, dx = q // 4, q % 4
                    k = ((x + (4 - dx)) & 3) * 2 + (core ^ dc)
                    where = pos[(which * blocks + j) * slots + k]
                    w = wbuf[q, which * blocks + j]
                    right.append(jnp.where(where >= 0, w, jnp.zeros_like(w)))
                    left.append(fbuf[jnp.maximum(where, 0)])
                part = jnp.dot(
                    jnp.concatenate(left, axis=1), jnp.concatenate(right, axis=0), preferred_element_type=F32
                )
                total = part if total is None else total + part
            return total

        def step(j, carry):
            gate = product(j, 0)
            up = product(j, 1)
            out[j] = (gate / (1.0 + jnp.exp(-gate)) * up).astype(BF)
            return carry

        lax.fori_loop(0, blocks, step, 0)

    return body


def down_kernel(hplan, wplan, n_h, n_w):
    def body(meta, hpos, lo, hi, *refs):
        hs, ws = refs[:n_h], refs[n_h : n_h + n_w]
        outs = refs[n_h + n_w : n_h + n_w + 8]
        hbuf, wbuf, acc, hsem, wsem = refs[n_h + n_w + 8 :]
        loads = []
        for i, (ref, row, q, first, count) in enumerate(wplan):
            src = ws[ref].at[pl.ds(row, count), :]
            loads.append(pltpu.make_async_copy(src, wbuf.at[q, pl.ds(first, count), :], wsem.at[i]))
        for i, (ref, first, count) in enumerate(hplan):
            loads.append(pltpu.make_async_copy(hs[ref], hbuf.at[pl.ds(first, count)], hsem.at[i]))
        for c in loads:
            c.start()
        for c in loads:
            c.wait()
        x, core, z = meta[0], meta[1], meta[2]
        for dz in (3, 5, 4, 2, 6, 1, 7, 0):

            def column(col, none, dz=dz):
                row = ((z + (8 - dz)) & 7) * 2 + col
                lane = pl.multiple_of(col * 128, 128)
                first, last = lo[row], hi[row]
                acc[...] = jnp.zeros_like(acc)

                def block(k):
                    tok = (k * 43) >> 7
                    q = (core ^ (tok & 1)) * 4 + ((x + 4 - (tok >> 1)) & 3)
                    at = pl.multiple_of(dz * 384 + (k - 3 * tok) * 128, 128)
                    return wbuf[q, pl.ds(at, 128), pl.ds(lane, 128)]

                def step(i, carry):
                    k0 = first + 2 * i
                    k1 = jnp.minimum(k0 + 1, 23)
                    w1 = block(k1)
                    w1 = jnp.where(k0 + 1 < last, w1, jnp.zeros_like(w1))
                    left = jnp.concatenate([hbuf[hpos[row * 24 + k0]], hbuf[hpos[row * 24 + k1]]], axis=1)
                    acc[...] += jnp.dot(
                        left, jnp.concatenate([block(k0), w1], axis=0), preferred_element_type=F32
                    )
                    return carry

                lax.fori_loop(0, (last - first + 1) // 2, step, 0)
                outs[dz][:, pl.ds(lane, 128)] = acc[...].astype(outs[dz].dtype)
                return none

            lax.fori_loop(0, 2, column, 0)

    return body


def on_device(tokens, gate_weight, up_weight, down_weight, gate_list, up_list, down_list):
    x, c, z, y = (lax.axis_index(a) for a in "xczy")
    rows = tokens.shape[0]
    rb = rows - RA
    blocks, slots = gate_list.shape
    meta = jnp.stack([x, c, z, y]).astype(jnp.int32)

    own = jnp.concatenate([gate_weight[:, 0], up_weight[:, 0]], axis=0)
    over_x = [own, shift(own, "x", 1), shift(own, "x", 2), shift(own, "x", -1)]
    both = 2 * blocks
    entries = [(v, slice(None), pl.ds(i * both, both)) for i, v in enumerate(over_x)]
    w_arrays = over_x + [shift(pack(entries, (4 * both, 128, 128)), "c", 1)]
    w_plan = [(min(q, 4), (q - min(q, 4)) * both, q, both) for q in range(8)]

    tok_y = {0: [tokens], 1: [shift(tokens, "y", 1)], 2: [shift(tokens, "y", 2)], 3: [shift(tokens, "y", -1)]}
    entries = rows_of([tokens], 0, RA, 0)
    for col in range(2):
        for k in range(3):
            entries.append((down_weight, (col, k), (pl.ds(RA + k * 128, 128), pl.ds(col * 128, 128))))
    up = down = pack(entries, (RA + 384, 256))
    ring_a = {0: [up]}
    for d in range(1, 4):
        up, down = shift(up, "z", 1), shift(down, "z", -1)
        ring_a[d], ring_a[8 - d] = [up], [down]
    ring_a[4] = [shift(up, "z", 1)]
    entries = sum((rows_of(tok_y[dy], RA, rows, dy * rb) for dy in range(4)), [])
    up = down = pack(entries, (4 * rb, 256))
    ring_b = {0: [up]}
    for d in range(1, 4):
        up, down = shift(up, "z", 1), shift(down, "z", -1)
        ring_b[d], ring_b[8 - d] = [up], [down]
    ring_b[4] = [shift(down, "z", -1)]

    arrays, feat_plan = [], []

    def use(parts, start, stop, piece, dst):
        for part, lo, count in cut(parts, start, stop):
            for ref, known in enumerate(arrays):
                if known is part:
                    break
            else:
                ref = len(arrays)
                arrays.append(part)
            feat_plan.append((ref, lo, count, piece, dst))
            dst += count

    for dy in range(4):
        use(tok_y[dy], 0, rows, dy, 0)
    for dz in range(1, 8):
        for dy in range(4):
            use(ring_b[dz], dy * rb, dy * rb + rb, dz * 4 + dy, RA)
    for tag, group in (("g", (1, 7, 2, 6)), ("g2", (3, 5, 4))):
        entries = sum((rows_of(ring_a[dz], 0, RA, i * RA) for i, dz in enumerate(group)), [])
        stack = pack(entries, (len(group) * RA, 256))
        one, three = shift(stack, "y", 1), shift(stack, "y", -1)
        two = shift(one, "y", 1) if tag == "g" else shift(stack, "y", 2)
        over_y = [[stack], [one], [two], [three]]
        for i, dz in enumerate(group):
            for dy in range(4):
                use(over_y[dy], i * RA, i * RA + RA, dz * 4 + dy, 0)

    pos, hpos, lo, hi = pl.pallas_call(
        tables,
        out_shape=tuple(jax.ShapeDtypeStruct((n,), jnp.int32) for n in (112, 384, 16, 16)),
        in_specs=[SMEM] * 4,
        out_specs=(SMEM,) * 4,
        name="tables",
    )(meta, gate_list, up_list, down_list)
    hidden = pl.pallas_call(
        hidden_kernel({"feat": feat_plan, "weight": w_plan}, len(arrays), len(w_arrays), blocks, slots),
        out_shape=jax.ShapeDtypeStruct((blocks, rows, 128), BF),
        in_specs=[SMEM, SMEM] + [ANY] * (len(arrays) + len(w_arrays)),
        out_specs=pl.BlockSpec(memory_space=pltpu.VMEM),
        scratch_shapes=[
            pltpu.VMEM((64, rows, 128), BF),
            pltpu.VMEM((8, 2 * blocks, 128, 128), BF),
            pltpu.SemaphoreType.DMA((2 * len(feat_plan),)),
            pltpu.SemaphoreType.DMA((len(w_plan),)),
        ],
        compiler_params=pltpu.CompilerParams(vmem_limit_bytes=56 * 1024 * 1024),
        name="gate_up",
    )(meta, pos, *arrays, *w_arrays)

    entries = sum((rows_of(ring_a[dz], RA, RA + 384, dz * 384) for dz in range(8)), [])
    down_own = pack(entries, (8 * 384, 256))
    one, three = shift(down_own, "x", 1), shift(down_own, "x", -1)
    low = shift(one[: 4 * 384], "x", 1)
    high = shift(three[4 * 384 :], "x", -1)
    full, part = 8 * 384, 4 * 384
    near = sum((rows_of([v], 0, full, i * full) for i, v in enumerate((down_own, one, three))), [])
    far = rows_of([low, high], 0, full, 0)
    over_c = (shift(pack(near, (3 * full, 256)), "c", 1), shift(pack(far, (full, 256)), "c", 1))
    d_arrays = [down_own, one, three, low, high, *over_c]
    d_plan = [
        (0, 0, 0, 0, full), (1, 0, 1, 0, full), (2, 0, 3, 0, full), (3, 0, 2, 0, part), (4, 0, 2, part, part),
        (5, 0, 4, 0, full), (5, full, 5, 0, full), (5, 2 * full, 7, 0, full), (6, 0, 6, 0, full),
    ]

    one, three = shift(hidden, "y", 1), shift(hidden, "y", -1)
    low, high = shift(one[:4], "y", 1), shift(three[4:], "y", -1)
    over_y = [[hidden], [one], [low, high], [three]]
    h_arrays, h_plan = [], []
    for dy in range(4):
        first = dy * blocks
        for part in over_y[dy]:
            h_plan.append((len(h_arrays), first, part.shape[0]))
            h_arrays.append(part)
            first += part.shape[0]

    part = pl.pallas_call(
        down_kernel(h_plan, d_plan, len(h_arrays), len(d_arrays)),
        out_shape=tuple(jax.ShapeDtypeStruct((rows, 256), F32 if dz in (0, 2, 6) else BF) for dz in range(8)),
        in_specs=[SMEM] * 4 + [ANY] * (len(h_arrays) + len(d_arrays)),
        out_specs=tuple(pl.BlockSpec(memory_space=pltpu.VMEM) for _ in range(8)),
        scratch_shapes=[
            pltpu.VMEM((NY * blocks, rows, 128), BF),
            pltpu.VMEM((8, 8 * 384, 256), BF),
            pltpu.VMEM((rows, 128), F32),
            pltpu.SemaphoreType.DMA((len(h_plan),)),
            pltpu.SemaphoreType.DMA((len(d_plan),)),
        ],
        compiler_params=pltpu.CompilerParams(vmem_limit_bytes=24 * 1024 * 1024),
        name="down",
    )(meta, hpos, lo, hi, *h_arrays, *d_arrays)

    got3 = shift(part[3], "z", -1)
    got5 = shift(part[5], "z", 1)
    got4 = shift(part[4], "z", -2)
    got1 = shift(part[1], "z", -1)
    got7 = shift(part[7], "z", 1)
    sum2 = part[2] + got3.astype(F32) + got4.astype(F32)
    sum6 = part[6] + got5.astype(F32)
    got2 = shift(sum2.astype(BF), "z", -2)
    got6 = shift(sum6.astype(BF), "z", 2)
    total = part[0] + got1.astype(F32) + got7.astype(F32) + got2.astype(F32) + got6.astype(F32)
    return total.astype(BF)


def solution(mesh):
    fine = Mesh(mesh.devices.reshape(NX, NC, NZ, NY), ("x", "c", "z", "y"))
    tok, wa = ("x", "c"), ("z", "y")
    placed = (
        P(tok, wa),
        P(wa, tok, None, None),
        P(wa, tok, None, None),
        P(wa, tok, None, None),
        P(wa, None),
        P(wa, None),
        P(),
    )

    return jax.shard_map(on_device, mesh=fine, in_specs=placed, out_specs=P(tok, wa), check_vma=False)
```

```python
import jax
import jax.numpy as jnp
from jax import lax
from jax.experimental import pallas as pl
from jax.experimental.pallas import tpu as pltpu
from jax.sharding import Mesh, PartitionSpec as P


NX, NC, NZ, NY = 4, 2, 8, 4
RA = 304
BF, F32 = jnp.bfloat16, jnp.float32
ANY = pl.BlockSpec(memory_space=pl.ANY)
SMEM = pl.BlockSpec(memory_space=pltpu.SMEM)


def shift(value, axis, by):
    size = {"x": NX, "c": NC, "z": NZ, "y": NY}[axis]
    return lax.ppermute(value, axis, [(i, (i + by) % size) for i in range(size)])


def cut(parts, start, stop):
    found, base = [], 0
    for part in parts:
        rows = part.shape[0]
        lo, hi = max(start, base), min(stop, base + rows)
        if lo < hi:
            found.append((part, lo - base, hi - lo))
        base += rows
    return found


def pack(pieces, rows):
    arrays = []
    for array, *_ in pieces:
        if not any(array is known for known in arrays):
            arrays.append(array)

    def body(*refs):
        out, sem = refs[-2:]
        copies = []
        for i, (array, at, count, row, lane, lanes) in enumerate(pieces):
            src = refs[[array is known for known in arrays].index(True)].at[at]
            dst = out.at[pl.ds(row, count), pl.ds(lane, lanes)]
            copies.append(pltpu.make_async_copy(src, dst, sem.at[i]))
        for c in copies:
            c.start()
        for c in copies:
            c.wait()

    return pl.pallas_call(
        body,
        out_shape=jax.ShapeDtypeStruct((rows, 256), BF),
        in_specs=[ANY] * len(arrays),
        out_specs=pl.BlockSpec(memory_space=pltpu.VMEM),
        scratch_shapes=[pltpu.SemaphoreType.DMA((len(pieces),))],
    )(*arrays)


def rows_of(parts, start, stop, row):
    out = []
    for part, lo, count in cut(parts, start, stop):
        out.append((part, (pl.ds(lo, count), slice(None)), count, row, 0, 256))
        row += count
    return out


def tables(meta, lists, downs, pos, hpos, first, last):
    z, y = meta[2], meta[3]
    base = z * 28

    def feature(r, carry):
        for i in range(8):
            f = lists[r * 8 + i]
            g = jnp.maximum(f, 0)
            owner = g >> 1
            piece = ((z + 8 - (owner >> 2)) & 7) * 4 + ((y + 4 - (owner & 3)) & 3)
            pos[r * 8 + i] = jnp.where(f >= 0, 2 * piece + (g & 1), -1)
        return carry

    lax.fori_loop(0, 14, feature, 0)

    def column(r, carry):
        row = (((r >> 1) * 4 + y) * 2 + (r & 1)) * 24
        below = upto = jnp.int32(0)
        for k in range(24):
            h = downs[row + k]
            local = h - base
            listed = (h >= 0).astype(jnp.int32)
            below += jnp.where(local < 0, listed, 0)
            upto += jnp.where(local < 28, listed, 0)
            local = jnp.clip(local, 0, 27)
            source = (local * 37) >> 8
            hpos[r * 24 + k] = ((y + 4 - source) & 3) * 7 + local - 7 * source
        first[r] = below
        last[r] = upto
        return carry

    lax.fori_loop(0, 16, column, 0)


def hidden_kernel(plan, n_feat, n_w, blocks, slots):
    def body(meta, pos, *refs):
        feats, weights = refs[:n_feat], refs[n_feat : n_feat + n_w]
        out, fbuf, wbuf, fsem, wsem = refs[n_feat + n_w :]
        copies = []
        for ref, lo, count, piece, dst in plan["feat"]:
            for h in range(2):
                copies.append(
                    pltpu.make_async_copy(
                        feats[ref].at[pl.ds(lo, count), pl.ds(h * 128, 128)],
                        fbuf.at[2 * piece + h, pl.ds(dst, count), :],
                        fsem.at[len(copies)],
                    )
                )
        loads = []
        for i, (ref, q, lo, count) in enumerate(plan["weight"]):
            loads.append(pltpu.make_async_copy(weights[ref], wbuf.at[q, pl.ds(lo, count)], wsem.at[i]))
        for c in loads + copies:
            c.start()
        x, core = meta[0], meta[1]
        for c in loads + copies:
            c.wait()

        def product(j, which):
            total = None
            for pair in range(slots // 2):
                left, right = [], []
                for q in (2 * pair, 2 * pair + 1):
                    dc, dx = q // 4, q % 4
                    k = ((x + (4 - dx)) & 3) * 2 + (core ^ dc)
                    where = pos[(which * blocks + j) * slots + k]
                    w = wbuf[q, which * blocks + j]
                    right.append(jnp.where(where >= 0, w, jnp.zeros_like(w)))
                    left.append(fbuf[jnp.maximum(where, 0)])
                part = jnp.dot(
                    jnp.concatenate(left, axis=1), jnp.concatenate(right, axis=0), preferred_element_type=F32
                )
                total = part if total is None else total + part
            return total

        def step(j, carry):
            gate = product(j, 0)
            up = product(j, 1)
            out[j] = (gate / (1.0 + jnp.exp(-gate)) * up).astype(BF)
            return carry

        lax.fori_loop(0, blocks, step, 0)

    return body


def down_kernel(hplan, wplan, n_h, n_w):
    def body(meta, hpos, lo, hi, *refs):
        hs, ws = refs[:n_h], refs[n_h : n_h + n_w]
        outs = refs[n_h + n_w : n_h + n_w + 8]
        hbuf, wbuf, acc, hsem, wsem = refs[n_h + n_w + 8 :]
        loads = []
        for i, (ref, q, first, count) in enumerate(wplan):
            loads.append(pltpu.make_async_copy(ws[ref], wbuf.at[q, pl.ds(first, count), :], wsem.at[i]))
        for i, (ref, first, count) in enumerate(hplan):
            loads.append(pltpu.make_async_copy(hs[ref], hbuf.at[pl.ds(first, count)], hsem.at[i]))
        for c in loads:
            c.start()
        for c in loads:
            c.wait()
        x, core, z = meta[0], meta[1], meta[2]
        for dz in (3, 5, 4, 2, 6, 1, 7, 0):
            for col in range(2):
                row = ((z + (8 - dz)) & 7) * 2 + col
                first, last = lo[row], hi[row]
                acc[...] = jnp.zeros_like(acc)

                def block(k):
                    tok = (k * 43) >> 7
                    q = (core ^ (tok & 1)) * 4 + ((x + 4 - (tok >> 1)) & 3)
                    at = pl.multiple_of(dz * 384 + (k - 3 * tok) * 128, 128)
                    return wbuf[q, pl.ds(at, 128), col * 128 : col * 128 + 128]

                def step(i, carry):
                    k0 = first + 2 * i
                    k1 = jnp.minimum(k0 + 1, 23)
                    w1 = block(k1)
                    w1 = jnp.where(k0 + 1 < last, w1, jnp.zeros_like(w1))
                    left = jnp.concatenate([hbuf[hpos[row * 24 + k0]], hbuf[hpos[row * 24 + k1]]], axis=1)
                    acc[...] += jnp.dot(
                        left, jnp.concatenate([block(k0), w1], axis=0), preferred_element_type=F32
                    )
                    return carry

                lax.fori_loop(0, (last - first + 1) // 2, step, 0)
                lanes = slice(col * 128, col * 128 + 128)
                outs[dz][:, lanes] = acc[...].astype(outs[dz].dtype)

    return body


def on_device(tokens, gate_weight, up_weight, down_weight, gate_list, up_list, down_list):
    x, c, z, y = (lax.axis_index(a) for a in "xczy")
    rows = tokens.shape[0]
    rb = rows - RA
    blocks, slots = gate_list.shape
    meta = jnp.stack([x, c, z, y]).astype(jnp.int32)

    own = jnp.concatenate([gate_weight[:, 0], up_weight[:, 0]], axis=0)
    over_x = [own, shift(own, "x", 1), shift(own, "x", 2), shift(own, "x", -1)]
    w_arrays = over_x + [shift(v, "c", 1) for v in over_x]
    w_plan = [(q, q, 0, 2 * blocks) for q in range(8)]

    tok_y = {0: [tokens], 1: [shift(tokens, "y", 1)], 2: [shift(tokens, "y", 2)], 3: [shift(tokens, "y", -1)]}
    entries = [(tokens, (pl.ds(0, RA), slice(None)), RA, 0, 0, 256)]
    for col in range(2):
        for k in range(3):
            entries.append((down_weight, (col, k), 128, RA + k * 128, col * 128, 128))
    up = down = pack(entries, RA + 384)
    ring_a = {0: [up]}
    for d in range(1, 4):
        up, down = shift(up, "z", 1), shift(down, "z", -1)
        ring_a[d], ring_a[8 - d] = [up], [down]
    ring_a[4] = [shift(up, "z", 1)]
    entries = sum((rows_of(tok_y[dy], RA, rows, dy * rb) for dy in range(4)), [])
    up = down = pack(entries, 4 * rb)
    ring_b = {0: [up]}
    for d in range(1, 4):
        up, down = shift(up, "z", 1), shift(down, "z", -1)
        ring_b[d], ring_b[8 - d] = [up], [down]
    ring_b[4] = [shift(down, "z", -1)]

    arrays, feat_plan = [], []

    def use(parts, start, stop, piece, dst):
        for part, lo, count in cut(parts, start, stop):
            for ref, known in enumerate(arrays):
                if known is part:
                    break
            else:
                ref = len(arrays)
                arrays.append(part)
            feat_plan.append((ref, lo, count, piece, dst))
            dst += count

    for dy in range(4):
        use(tok_y[dy], 0, rows, dy, 0)
    for dz in range(1, 8):
        for dy in range(4):
            use(ring_b[dz], dy * rb, dy * rb + rb, dz * 4 + dy, RA)
    for tag, group in (("a", (1, 7)), ("b", (2, 6)), ("g2", (3, 5, 4))):
        entries = sum((rows_of(ring_a[dz], 0, RA, i * RA) for i, dz in enumerate(group)), [])
        stack = pack(entries, len(group) * RA)
        one, three = shift(stack, "y", 1), shift(stack, "y", -1)
        two = {
            "a": lambda: shift(one, "y", 1), "b": lambda: shift(three, "y", -1), "g2": lambda: shift(stack, "y", 2)
        }[tag]()
        over_y = [[stack], [one], [two], [three]]
        for i, dz in enumerate(group):
            for dy in range(4):
                use(over_y[dy], i * RA, i * RA + RA, dz * 4 + dy, 0)

    lists = jnp.concatenate([gate_list, up_list], axis=0).reshape(-1)
    pos, hpos, lo, hi = pl.pallas_call(
        tables,
        out_shape=tuple(jax.ShapeDtypeStruct((n,), jnp.int32) for n in (112, 384, 16, 16)),
        in_specs=[SMEM] * 3,
        out_specs=(SMEM,) * 4,
        name="tables",
    )(meta, lists, down_list.reshape(-1))
    hidden = pl.pallas_call(
        hidden_kernel({"feat": feat_plan, "weight": w_plan}, len(arrays), len(w_arrays), blocks, slots),
        out_shape=jax.ShapeDtypeStruct((blocks, rows, 128), BF),
        in_specs=[SMEM, SMEM] + [ANY] * (len(arrays) + len(w_arrays)),
        out_specs=pl.BlockSpec(memory_space=pltpu.VMEM),
        scratch_shapes=[
            pltpu.VMEM((64, rows, 128), BF),
            pltpu.VMEM((8, 2 * blocks, 128, 128), BF),
            pltpu.SemaphoreType.DMA((2 * len(feat_plan),)),
            pltpu.SemaphoreType.DMA((len(w_plan),)),
        ],
        compiler_params=pltpu.CompilerParams(vmem_limit_bytes=20 * 1024 * 1024),
        name="gate_up",
    )(meta, pos, *arrays, *w_arrays)

    entries = sum((rows_of(ring_a[dz], RA, RA + 384, dz * 384) for dz in range(8)), [])
    down_own = pack(entries, 8 * 384)
    one, three = shift(down_own, "x", 1), shift(down_own, "x", -1)
    low = shift(one[: 4 * 384], "x", 1)
    high = shift(three[4 * 384 :], "x", -1)
    d_arrays = [down_own, one, three, low, high]
    d_arrays += [shift(v, "c", 1) for v in d_arrays]
    d_plan = []
    for dc in range(2):
        for i, (dx, first) in enumerate(((0, 0), (1, 0), (3, 0), (2, 0), (2, 4 * 384))):
            d_plan.append((dc * 5 + i, dc * 4 + dx, first, d_arrays[i].shape[0]))

    one, three = shift(hidden, "y", 1), shift(hidden, "y", -1)
    low, high = shift(one[:4], "y", 1), shift(three[4:], "y", -1)
    over_y = [[hidden], [one], [low, high], [three]]
    h_arrays, h_plan = [], []
    for dy in range(4):
        first = dy * blocks
        for part in over_y[dy]:
            h_plan.append((len(h_arrays), first, part.shape[0]))
            h_arrays.append(part)
            first += part.shape[0]

    part = pl.pallas_call(
        down_kernel(h_plan, d_plan, len(h_arrays), len(d_arrays)),
        out_shape=tuple(jax.ShapeDtypeStruct((rows, 256), F32 if dz in (0, 2, 6) else BF) for dz in range(8)),
        in_specs=[SMEM] * 4 + [ANY] * (len(h_arrays) + len(d_arrays)),
        out_specs=tuple(pl.BlockSpec(memory_space=pltpu.VMEM) for _ in range(8)),
        scratch_shapes=[
            pltpu.VMEM((NY * blocks, rows, 128), BF),
            pltpu.VMEM((8, 8 * 384, 256), BF),
            pltpu.VMEM((rows, 128), F32),
            pltpu.SemaphoreType.DMA((len(h_plan),)),
            pltpu.SemaphoreType.DMA((len(d_plan),)),
        ],
        compiler_params=pltpu.CompilerParams(vmem_limit_bytes=24 * 1024 * 1024),
        name="down",
    )(meta, hpos, lo, hi, *h_arrays, *d_arrays)

    half = rows // 2
    got3 = shift(part[3], "z", -1)
    got5 = shift(part[5], "z", 1)
    got4a = shift(part[4][:half], "z", -2)
    got4b = shift(part[4][half:], "z", 2)
    got1 = shift(part[1], "z", -1)
    got7 = shift(part[7], "z", 1)
    zero = jnp.zeros((half, 256), F32)
    sum2 = part[2] + got3.astype(F32) + jnp.concatenate([got4a.astype(F32), zero], axis=0)
    sum6 = part[6] + got5.astype(F32) + jnp.concatenate([zero, got4b.astype(F32)], axis=0)
    got2 = shift(sum2.astype(BF), "z", -2)
    got6 = shift(sum6.astype(BF), "z", 2)
    total = part[0] + got1.astype(F32) + got7.astype(F32) + got2.astype(F32) + got6.astype(F32)
    return total.astype(BF)


def solution(mesh):
    fine = Mesh(mesh.devices.reshape(NX, NC, NZ, NY), ("x", "c", "z", "y"))
    tok, wa = ("x", "c"), ("z", "y")
    placed = (
        P(tok, wa),
        P(wa, tok, None, None),
        P(wa, tok, None, None),
        P(wa, tok, None, None),
        P(wa, None),
        P(wa, None),
        P(),
    )

    return jax.shard_map(on_device, mesh=fine, in_specs=placed, out_specs=P(tok, wa), check_vma=False)
```

```python
import jax
import jax.numpy as jnp
from jax import lax
from jax.experimental import pallas as pl
from jax.experimental.pallas import tpu as pltpu
from jax.sharding import Mesh, PartitionSpec as P


NX, NC, NZ, NY = 4, 2, 8, 4
RA = 288
BF, F32 = jnp.bfloat16, jnp.float32
ANY = pl.BlockSpec(memory_space=pl.ANY)
SMEM = pl.BlockSpec(memory_space=pltpu.SMEM)


def shift(value, axis, by):
    size = {"x": NX, "c": NC, "z": NZ, "y": NY}[axis]
    return lax.ppermute(value, axis, [(i, (i + by) % size) for i in range(size)])


def cut(parts, start, stop):
    found, base = [], 0
    for part in parts:
        rows = part.shape[0]
        lo, hi = max(start, base), min(stop, base + rows)
        if lo < hi:
            found.append((part, lo - base, hi - lo))
        base += rows
    return found


def pack(pieces, shape):
    arrays = []
    for array, *_ in pieces:
        if not any(array is known for known in arrays):
            arrays.append(array)

    def body(*refs):
        out, sem = refs[-2:]
        copies = []
        for i, (array, at, to) in enumerate(pieces):
            src = refs[[array is known for known in arrays].index(True)].at[at]
            copies.append(pltpu.make_async_copy(src, out.at[to], sem.at[i]))
        for c in copies:
            c.start()
        for c in copies:
            c.wait()

    return pl.pallas_call(
        body,
        out_shape=jax.ShapeDtypeStruct(shape, BF),
        in_specs=[ANY] * len(arrays),
        out_specs=pl.BlockSpec(memory_space=pltpu.VMEM),
        scratch_shapes=[pltpu.SemaphoreType.DMA((len(pieces),))],
    )(*arrays)


def rows_of(parts, start, stop, row):
    out = []
    for part, lo, count in cut(parts, start, stop):
        out.append((part, (pl.ds(lo, count), slice(None)), (pl.ds(row, count), slice(None))))
        row += count
    return out


def tables(meta, gates, ups, downs, pos, hpos, first, last):
    z, y = meta[2], meta[3]
    base = z * 28

    def feature(r, carry):
        for which, lists in enumerate((gates, ups)):
            for i in range(8):
                f = lists[r, i]
                g = jnp.maximum(f, 0)
                owner = g >> 1
                piece = ((z + 8 - (owner >> 2)) & 7) * 4 + ((y + 4 - (owner & 3)) & 3)
                pos[(which * 7 + r) * 8 + i] = jnp.where(f >= 0, 2 * piece + (g & 1), -1)
        return carry

    lax.fori_loop(0, 7, feature, 0)

    def column(r, carry):
        row = ((r >> 1) * 4 + y) * 2 + (r & 1)
        below = upto = jnp.int32(0)
        for k in range(24):
            h = downs[row, k]
            local = h - base
            listed = (h >= 0).astype(jnp.int32)
            below += jnp.where(local < 0, listed, 0)
            upto += jnp.where(local < 28, listed, 0)
            local = jnp.clip(local, 0, 27)
            source = (local * 37) >> 8
            hpos[r * 24 + k] = ((y + 4 - source) & 3) * 7 + local - 7 * source
        first[r] = below
        last[r] = upto
        return carry

    lax.fori_loop(0, 16, column, 0)


def hidden_kernel(plan, n_feat, n_w, blocks, slots):
    def body(meta, pos, *refs):
        feats, weights = refs[:n_feat], refs[n_feat : n_feat + n_w]
        out, fbuf, wbuf, sums, fsem, wsem = refs[n_feat + n_w :]
        copies = []
        for ref, lo, count, piece, dst in plan["feat"]:
            copies.append(
                pltpu.make_async_copy(
                    feats[ref].at[pl.ds(lo, count), :],
                    fbuf.at[piece, pl.ds(dst, count), :],
                    fsem.at[len(copies)],
                )
            )
        loads = []
        for i, (ref, row, q, count) in enumerate(plan["weight"]):
            loads.append(pltpu.make_async_copy(weights[ref].at[pl.ds(row, count)], wbuf.at[q], wsem.at[i]))
        for c in loads + copies:
            c.start()
        x, core = meta[0], meta[1]
        for c in loads + copies:
            c.wait()

        def product(j, which):
            total = None
            for pair in range(slots // 2):
                left, right = [], []
                for q in (2 * pair, 2 * pair + 1):
                    dc, dx = q // 4, q % 4
                    k = ((x + (4 - dx)) & 3) * 2 + (core ^ dc)
                    where = pos[(which * blocks + j) * slots + k]
                    w = wbuf[q, which * blocks + j]
                    right.append(jnp.where(where >= 0, w, jnp.zeros_like(w)))
                    at = jnp.maximum(where, 0)
                    left.append(fbuf[at >> 1, :, pl.ds(pl.multiple_of((at & 1) * 128, 128), 128)])
                part = jnp.dot(
                    jnp.concatenate(left, axis=1), jnp.concatenate(right, axis=0), preferred_element_type=F32
                )
                total = part if total is None else total + part
            return total

        def step(j, carry):

            def one(which, none):
                sums[which] = product(j, which)
                return none

            lax.fori_loop(0, 2, one, 0)
            gate, up = sums[0], sums[1]
            out[j] = (gate / (1.0 + jnp.exp(-gate)) * up).astype(BF)
            return carry

        lax.fori_loop(0, blocks, step, 0)

    return body


def down_kernel(hplan, wplan, n_h, n_w):
    def body(meta, hpos, lo, hi, *refs):
        hs, ws = refs[:n_h], refs[n_h : n_h + n_w]
        outs = refs[n_h + n_w : n_h + n_w + 8]
        hbuf, wbuf, acc, hsem, wsem = refs[n_h + n_w + 8 :]
        loads = []
        for i, (ref, row, q, first, count) in enumerate(wplan):
            src = ws[ref].at[pl.ds(row, count), :]
            loads.append(pltpu.make_async_copy(src, wbuf.at[q, pl.ds(first, count), :], wsem.at[i]))
        for i, (ref, first, count) in enumerate(hplan):
            loads.append(pltpu.make_async_copy(hs[ref], hbuf.at[pl.ds(first, count)], hsem.at[i]))
        for c in loads:
            c.start()
        for c in loads:
            c.wait()
        x, core, z = meta[0], meta[1], meta[2]
        for dz in (3, 5, 4, 2, 6, 1, 7, 0):

            def column(col, none, dz=dz):
                row = ((z + (8 - dz)) & 7) * 2 + col
                lane = pl.multiple_of(col * 128, 128)
                first, last = lo[row], hi[row]
                acc[...] = jnp.zeros_like(acc)

                def block(k):
                    tok = (k * 43) >> 7
                    q = (core ^ (tok & 1)) * 4 + ((x + 4 - (tok >> 1)) & 3)
                    at = pl.multiple_of(dz * 384 + (k - 3 * tok) * 128, 128)
                    return wbuf[q, pl.ds(at, 128), pl.ds(lane, 128)]

                def step(i, carry):
                    k0 = first + 2 * i
                    k1 = jnp.minimum(k0 + 1, 23)
                    w1 = block(k1)
                    w1 = jnp.where(k0 + 1 < last, w1, jnp.zeros_like(w1))
                    left = jnp.concatenate([hbuf[hpos[row * 24 + k0]], hbuf[hpos[row * 24 + k1]]], axis=1)
                    acc[...] += jnp.dot(
                        left, jnp.concatenate([block(k0), w1], axis=0), preferred_element_type=F32
                    )
                    return carry

                lax.fori_loop(0, (last - first + 1) // 2, step, 0)
                outs[dz][:, pl.ds(lane, 128)] = acc[...].astype(outs[dz].dtype)
                return none

            lax.fori_loop(0, 2, column, 0)

    return body


def on_device(tokens, gate_weight, up_weight, down_weight, gate_list, up_list, down_list):
    x, c, z, y = (lax.axis_index(a) for a in "xczy")
    rows = tokens.shape[0]
    rb = rows - RA
    blocks, slots = gate_list.shape
    meta = jnp.stack([x, c, z, y]).astype(jnp.int32)

    own = jnp.concatenate([gate_weight[:, 0], up_weight[:, 0]], axis=0)
    over_x = [own, shift(own, "x", 1), shift(own, "x", 2), shift(own, "x", -1)]
    both = 2 * blocks
    entries = [(v, slice(None), pl.ds(i * both, both)) for i, v in enumerate(over_x)]
    w_arrays = over_x + [shift(pack(entries, (4 * both, 128, 128)), "c", 1)]
    w_plan = [(min(q, 4), (q - min(q, 4)) * both, q, both) for q in range(8)]

    tok_y = {0: [tokens], 1: [shift(tokens, "y", 1)], 2: [shift(tokens, "y", 2)], 3: [shift(tokens, "y", -1)]}
    entries = rows_of([tokens], 0, RA, 0)
    for col in range(2):
        for k in range(3):
            entries.append((down_weight, (col, k), (pl.ds(RA + k * 128, 128), pl.ds(col * 128, 128))))
    up = down = pack(entries, (RA + 384, 256))
    ring_a = {0: [up]}
    for d in range(1, 4):
        up, down = shift(up, "z", 1), shift(down, "z", -1)
        ring_a[d], ring_a[8 - d] = [up], [down]
    ring_a[4] = [shift(up, "z", 1)]
    entries = sum((rows_of(tok_y[dy], RA, rows, dy * rb) for dy in range(4)), [])
    up = down = pack(entries, (4 * rb, 256))
    ring_b = {0: [up]}
    for d in range(1, 4):
        up, down = shift(up, "z", 1), shift(down, "z", -1)
        ring_b[d], ring_b[8 - d] = [up], [down]
    ring_b[4] = [shift(down, "z", -1)]

    arrays, feat_plan = [], []

    def use(parts, start, stop, piece, dst):
        for part, lo, count in cut(parts, start, stop):
            for ref, known in enumerate(arrays):
                if known is part:
                    break
            else:
                ref = len(arrays)
                arrays.append(part)
            feat_plan.append((ref, lo, count, piece, dst))
            dst += count

    for dy in range(4):
        use(tok_y[dy], 0, rows, dy, 0)
    for dz in range(1, 8):
        for dy in range(4):
            use(ring_b[dz], dy * rb, dy * rb + rb, dz * 4 + dy, RA)
    for tag, group in (("g", (1, 7, 2, 6)), ("g2", (3, 5, 4))):
        entries = sum((rows_of(ring_a[dz], 0, RA, i * RA) for i, dz in enumerate(group)), [])
        stack = pack(entries, (len(group) * RA, 256))
        one, three = shift(stack, "y", 1), shift(stack, "y", -1)
        two = shift(one, "y", 1) if tag == "g" else shift(stack, "y", 2)
        over_y = [[stack], [one], [two], [three]]
        for i, dz in enumerate(group):
            for dy in range(4):
                use(over_y[dy], i * RA, i * RA + RA, dz * 4 + dy, 0)

    pos, hpos, lo, hi = pl.pallas_call(
        tables,
        out_shape=tuple(jax.ShapeDtypeStruct((n,), jnp.int32) for n in (112, 384, 16, 16)),
        in_specs=[SMEM] * 4,
        out_specs=(SMEM,) * 4,
        name="tables",
    )(meta, gate_list, up_list, down_list)
    hidden = pl.pallas_call(
        hidden_kernel({"feat": feat_plan, "weight": w_plan}, len(arrays), len(w_arrays), blocks, slots),
        out_shape=jax.ShapeDtypeStruct((blocks, rows, 128), BF),
        in_specs=[SMEM, SMEM] + [ANY] * (len(arrays) + len(w_arrays)),
        out_specs=pl.BlockSpec(memory_space=pltpu.VMEM),
        scratch_shapes=[
            pltpu.VMEM((32, rows, 256), BF),
            pltpu.VMEM((8, 2 * blocks, 128, 128), BF),
            pltpu.VMEM((2, rows, 128), F32),
            pltpu.SemaphoreType.DMA((len(feat_plan),)),
            pltpu.SemaphoreType.DMA((len(w_plan),)),
        ],
        compiler_params=pltpu.CompilerParams(vmem_limit_bytes=56 * 1024 * 1024),
        name="gate_up",
    )(meta, pos, *arrays, *w_arrays)

    entries = sum((rows_of(ring_a[dz], RA, RA + 384, dz * 384) for dz in range(8)), [])
    down_own = pack(entries, (8 * 384, 256))
    one, three = shift(down_own, "x", 1), shift(down_own, "x", -1)
    first_half, second_half = one[: 4 * 384], three[4 * 384 :]
    low = shift(first_half, "x", 1)
    high = shift(second_half, "x", -1)
    full, part = 8 * 384, 4 * 384
    near = sum((rows_of([v], 0, full, i * full) for i, v in enumerate((down_own, one, three))), [])
    far = rows_of([low, high], 0, full, 0)
    over_c = (shift(pack(near, (3 * full, 256)), "c", 1), shift(pack(far, (full, 256)), "c", 1))
    d_arrays = [down_own, one, three, low, high, *over_c]
    d_plan = [
        (0, 0, 0, 0, full), (1, 0, 1, 0, full), (2, 0, 3, 0, full), (3, 0, 2, 0, part), (4, 0, 2, part, part),
        (5, 0, 4, 0, full), (5, full, 5, 0, full), (5, 2 * full, 7, 0, full), (6, 0, 6, 0, full),
    ]

    one, three = shift(hidden, "y", 1), shift(hidden, "y", -1)
    over_y = [[hidden], [one], [shift(hidden, "y", 2)], [three]]
    h_arrays, h_plan = [], []
    for dy in range(4):
        first = dy * blocks
        for part in over_y[dy]:
            h_plan.append((len(h_arrays), first, part.shape[0]))
            h_arrays.append(part)
            first += part.shape[0]

    part = pl.pallas_call(
        down_kernel(h_plan, d_plan, len(h_arrays), len(d_arrays)),
        out_shape=tuple(jax.ShapeDtypeStruct((rows, 256), F32 if dz in (0, 2, 6) else BF) for dz in range(8)),
        in_specs=[SMEM] * 4 + [ANY] * (len(h_arrays) + len(d_arrays)),
        out_specs=tuple(pl.BlockSpec(memory_space=pltpu.VMEM) for _ in range(8)),
        scratch_shapes=[
            pltpu.VMEM((NY * blocks, rows, 128), BF),
            pltpu.VMEM((8, 8 * 384, 256), BF),
            pltpu.VMEM((rows, 128), F32),
            pltpu.SemaphoreType.DMA((len(h_plan),)),
            pltpu.SemaphoreType.DMA((len(d_plan),)),
        ],
        compiler_params=pltpu.CompilerParams(vmem_limit_bytes=24 * 1024 * 1024),
        name="down",
    )(meta, hpos, lo, hi, *h_arrays, *d_arrays)

    got3 = shift(part[3], "z", -1)
    got5 = shift(part[5], "z", 1)
    half = rows // 2
    got4a = shift(part[4][:half], "z", -2)
    got4b = shift(part[4][half:], "z", 2)
    got1 = shift(part[1], "z", -1)
    got7 = shift(part[7], "z", 1)
    zero = jnp.zeros((half, 256), F32)
    sum2 = part[2] + got3.astype(F32) + jnp.concatenate([got4a.astype(F32), zero], axis=0)
    sum6 = part[6] + got5.astype(F32) + jnp.concatenate([zero, got4b.astype(F32)], axis=0)
    got2 = shift(sum2.astype(BF), "z", -2)
    got6 = shift(sum6.astype(BF), "z", 2)
    total = part[0] + got1.astype(F32) + got7.astype(F32) + got2.astype(F32) + got6.astype(F32)
    return total.astype(BF)


def solution(mesh):
    fine = Mesh(mesh.devices.reshape(NX, NC, NZ, NY), ("x", "c", "z", "y"))
    tok, wa = ("x", "c"), ("z", "y")
    placed = (
        P(tok, wa),
        P(wa, tok, None, None),
        P(wa, tok, None, None),
        P(wa, tok, None, None),
        P(wa, None),
        P(wa, None),
        P(),
    )

    return jax.shard_map(on_device, mesh=fine, in_specs=placed, out_specs=P(tok, wa), check_vma=False)
```
